32 devices in a mesh: groups: 2 (over x), dev: 8 (over z, y), sub: 2 (over core).
Axes of the slice: x: 2, y: 2, z: 4, core: 2. Of those that a mesh axis runs over, the one named last changes fastest.
Arguments:
- hidden: bfloat16 [128, 6144], P(('groups', 'dev')), parts along dimension 0, may hold values from -6 to 6
- query: bfloat16 [128, 48, 128], P(('groups', 'dev'), 'sub'), parts along dimension 0, may hold values from -180 to 180
- cache_keys: bfloat16 [128, 8, 64, 128], P(('groups', 'dev'), 'sub'), parts along dimension 0, may hold values from -6 to 6
- cache_values: bfloat16 [128, 8, 64, 128], P(('groups', 'dev'), 'sub'), parts along dimension 0, may hold values from -6 to 6
- lengths: int32 [128], P(('groups', 'dev')), parts along dimension 0, may hold values from 16 to 64
- out_proj: bfloat16 [6144, 6144], P('sub', 'dev'), may hold values from -0.078125 to 0.078125
- norm_gain: float32 [6144], replicated, may hold values from 0.1 to 1.9
- router: bfloat16 [6144, 4], replicated, may hold values from -0.078125 to 0.078125
- low_factor: bfloat16 [6144, 256], P('sub'), may hold values from -0.078125 to 0.078125
- gate_weight: bfloat16 [6144, 32768], P(None, ('dev', 'sub')), may hold values from -0.078125 to 0.078125
- up_weight: bfloat16 [6144, 32768], P(None, ('dev', 'sub')), may hold values from -0.078125 to 0.078125
- down_weight: bfloat16 [32768, 6144], P(('dev', 'sub')), may hold values from -0.0625 to 0.0625
- gate_low: bfloat16 [256, 32768], P(None, ('dev', 'sub')), may hold values from -0.375 to 0.375
- up_low: bfloat16 [256, 32768], P(None, ('dev', 'sub')), may hold values from -0.375 to 0.375
- experts: int32 [128, 2], P(('groups', 'dev')), parts along dimension 0, may hold values from 0 to 3, all different within a row; in each aligned block of 8 rows (0 to 7, 8 to 15, ...) at most 6 rows name the same one
Outputs:
- layer_out: bfloat16 [128, 6144], P(('groups', 'dev')), parts along dimension 0
- mixture: float32 [128, 6144], P(('groups', 'dev')), parts along dimension 0
The draws below stay inside these ranges and needn't reach their ends.
There are 2 independent parts, one for each index of `groups`. The reference program is written for one: setup_inputs(seed, part) draws one part's arguments, and reference() takes and returns one part's arrays. A program takes and returns all parts, laid end to end along the dimension named above; an argument that names none is the same for every part. Nothing has to cross between parts.
Inputs may be any that keep to these rules, and one draw needn't show every extreme that they name: Each row names two different experts. Among the 8 requests of one device no expert is named more than 6 times, and that bound is reached on some device.
All inputs are finite; a program needn't handle non-finite values.
Results may differ from the reference program's by a relative error of at most 0.015.
Values may be sent and summed in bfloat16 or wider, within the bound.
A program may use at most 128 MiB of HBM per device.

```python
import math
import jax
import jax.numpy as jnp
import numpy as np
from jax import lax

D = 6144
QH = 48
KVH = 8
HD = 128
EXPERTS = 4
FF = 8192
RANK = 256
REQ_DEV = 8
SPAN = 64
CAP = 6
REQ = 64


def drawn_pair(key):
    streams = jax.random.split(jax.random.fold_in(key, 31), 2)
    query_draw = jnp.clip(jax.random.normal(streams[0], (REQ, QH, HD), jnp.float32), -6.0, 6.0)
    key_draw = jnp.clip(jax.random.normal(streams[1], (REQ, KVH, SPAN, HD), jnp.float32), -6.0, 6.0)
    return (query_draw, key_draw)


def draw_query(key, part):
    return drawn_pair(key)[0].astype(jnp.bfloat16)


def draw_cache_keys(key, part):
    return drawn_pair(key)[1].astype(jnp.bfloat16)


def set_ends(array, key, least, high):
    spot = [jax.random.randint(jax.random.fold_in(key, axis), (), 0, length) for axis, length in enumerate(array.shape)]
    main_axis = array.shape.index(max(array.shape))
    next_to = spot[:main_axis] + [(spot[main_axis] + 1) % array.shape[main_axis]] + spot[main_axis + 1:]
    return array.at[tuple(spot)].set(least).at[tuple(next_to)].set(high)


def levels(rng, shape, cuts, smallest, top_value):
    def one(axis_at, shards_of):
        draws = jax.random.uniform(jax.random.fold_in(jax.random.fold_in(rng, 6), axis_at), (shards_of,), jnp.float32, smallest / len(cuts), top_value / len(cuts))
        return jnp.repeat(jnp.exp(draws), shape[axis_at] // shards_of).reshape((-1,) + (1,) * (len(shape) - axis_at - 1))

    loudness = one(*cuts[0])
    for cut in cuts[1:]:
        loudness = loudness * one(*cut)
    return loudness


def assign_block(key, own, number, rows, amount, top, most, slope):
    sequence = jax.random.permutation(key, amount)
    heavy_load, usual = portions_of(amount, rows * top, most, slope, True), portions_of(amount, rows * top, most, slope, False)
    places = jnp.arange(amount)

    def named(sizes, offset_by):
        used = int((sizes > 0).sum())
        fixed = max(1, used // 4)
        shifted = fixed + (places - fixed + offset_by * (used - fixed)) % max(1, amount - fixed)
        return jnp.zeros((amount,), jnp.int32).at[sequence[jnp.where(places < fixed, places, shifted)]].set(jnp.asarray(sizes, jnp.int32))

    sizes = jnp.where(number % 4 == 0, named(heavy_load, number // 4), named(usual, number - number // 4 - 1))
    mixed = jax.random.permutation(jax.random.fold_in(own, 3), amount)
    source_of, sink = mixed[0:amount // 2 * 2:2], mixed[1:amount // 2 * 2:2]
    room = jnp.minimum(sizes[source_of] - 1, most - sizes[sink]) // 2
    room = jnp.where((source_of == sequence[0]) | (sink == sequence[0]) | (sizes[sink] == 0), 0, jnp.maximum(room, 0))
    shifted = jax.random.randint(jax.random.fold_in(own, 4), (amount // 2,), 0, 1 << 20) % (room + 1)
    sizes = sizes.at[source_of].add(-shifted).at[sink].add(shifted)
    items = jnp.searchsorted(jnp.cumsum(sizes), jnp.arange(rows * top), side="right").astype(jnp.int32)
    table = items.reshape(top, rows).T
    table = table[jax.random.permutation(jax.random.fold_in(own, 1), rows)]
    offset_by = jax.random.randint(jax.random.fold_in(own, 2), (rows, 1), 0, top)
    return jnp.take_along_axis(table, (jnp.arange(top)[None, :] + offset_by) % top, axis=1)


def portions_of(count, total, limit, skew, full):
    portions = [(1 << 20) // math.isqrt(rank ** skew) + 1 for rank in range(1, count + 1)]
    largest = limit if full else min(limit, max(-(-total // count), total * portions[0] // sum(portions)))
    least = 1 if total - largest >= count - 1 else 0
    holding, surplus = [largest] + [least] * (count - 1), total - largest - least * (count - 1)
    while surplus > 0:
        free = [i for i in range(1, count) if holding[i] < largest] or [i for i in range(1, count) if holding[i] < limit]
        pool, budget = sum([portions[i] for i in free]), surplus
        for i in free:
            extra = min(limit - holding[i], max(1, budget * portions[i] // pool), surplus)
            holding[i] = holding[i] + extra
            surplus = surplus - extra
    return np.array(holding)


def scatter_about(rng, shape, scale, reach, cuts=(), kind=jnp.bfloat16):
    array = jax.random.normal(rng, shape, jnp.float32) * scale
    if len(cuts) > 0:
        array = levels(rng, shape, cuts, -0.22, 0.18) * array
    return jnp.clip(array, min=-reach, max=reach).astype(kind)


def setup_inputs(seed: int = 0, part: int = 0) -> dict:
    arg_keys = jax.random.split(jax.random.key(seed), 16)
    part_keys = jax.random.split(jax.random.fold_in(arg_keys[15], part), 16)
    hidden = scatter_about(part_keys[0], (REQ, D), 1.0, 6.0, ((0, 8),))
    query = draw_query(jax.random.fold_in(jax.random.fold_in(arg_keys[15], part), 71), part)
    cache_keys = draw_cache_keys(jax.random.fold_in(jax.random.fold_in(arg_keys[15], part), 71), part)
    cache_values = scatter_about(part_keys[3], (REQ, KVH, SPAN, HD), 1.0, 6.0, ((0, 8), (1, 2)))
    lengths = set_ends(jax.random.randint(part_keys[4], (REQ,), SPAN // 4, SPAN + 1), jax.random.fold_in(part_keys[4], 1), SPAN // 4, SPAN).astype(jnp.int32)
    out_proj = scatter_about(arg_keys[5], (QH * HD, D), (QH * HD) ** -0.5, 0.078125, ((0, 2), (1, 8)))
    norm_gain = jnp.clip(1.0 + 0.18 * jax.random.normal(arg_keys[6], (D,), jnp.float32), 0.1, 1.9)
    router = scatter_about(arg_keys[7], (D, EXPERTS), D ** -0.5, 0.078125)
    low_factor = scatter_about(arg_keys[8], (D, RANK), D ** -0.5, 0.078125, ((0, 2),))
    gate_weight = scatter_about(arg_keys[9], (D, EXPERTS * FF), D ** -0.5, 0.078125, ((1, 16),))
    up_weight = scatter_about(arg_keys[10], (D, EXPERTS * FF), D ** -0.5, 0.078125, ((1, 16),))
    down_weight = scatter_about(arg_keys[11], (EXPERTS * FF, D), FF ** -0.5, 0.0625, ((0, 16),))
    gate_low = scatter_about(arg_keys[12], (RANK, EXPERTS * FF), RANK ** -0.5, 0.375, ((1, 16),))
    up_low = scatter_about(arg_keys[13], (RANK, EXPERTS * FF), RANK ** -0.5, 0.375, ((1, 16),))
    experts_keys = jax.random.split(jax.random.fold_in(part_keys[14], 1), REQ // REQ_DEV)
    experts_turns = jax.random.permutation(jax.random.fold_in(part_keys[14], 3), REQ // REQ_DEV)
    experts = jax.vmap(lambda own, number: assign_block(jax.random.fold_in(part_keys[14], 2), own, number, REQ_DEV, EXPERTS, 2, CAP, 2))(experts_keys, experts_turns).reshape((REQ, 2))
    return dict(hidden=hidden, query=query, cache_keys=cache_keys, cache_values=cache_values, lengths=lengths, out_proj=out_proj, norm_gain=norm_gain, router=router, low_factor=low_factor, gate_weight=gate_weight, up_weight=up_weight, down_weight=down_weight, gate_low=gate_low, up_low=up_low, experts=experts)


EPSILON = 1e-05

def expert_shard(row_block, low_rank, gate_weight, up_weight, down_weight, gate_low, up_low):
    gate_sum = jnp.dot(row_block, gate_weight, preferred_element_type=jnp.float32) + jnp.dot(low_rank, gate_low, preferred_element_type=jnp.float32)
    up_sum = jnp.dot(row_block, up_weight, preferred_element_type=jnp.float32) + jnp.dot(low_rank, up_low, preferred_element_type=jnp.float32)
    inner_act = (jax.nn.silu(gate_sum) * up_sum).astype(jnp.bfloat16)
    return jnp.dot(inner_act, down_weight, preferred_element_type=jnp.float32)

def route_gates(normed, router, experts):
    logits = jnp.dot(normed, router, preferred_element_type=jnp.float32)
    labels = lax.broadcasted_iota(jnp.int32, (1, 1, router.shape[1]), 2)
    picked = (experts[:, :, None] == labels).astype(jnp.float32)
    chosen = lax.optimization_barrier(jnp.sum(logits[:, None, :] * picked, axis=-1))
    leading = jax.nn.sigmoid(chosen[:, 0] - chosen[:, 1])
    return jnp.stack([leading, 1.0 - leading], axis=-1)

def reference(hidden, query, cache_keys, cache_values, lengths, out_proj, norm_gain, router, low_factor, gate_weight, up_weight, down_weight, gate_low, up_low, experts):
    heads_per_kv = QH // KVH
    grouped = query.astype(jnp.float32).reshape(REQ, KVH, heads_per_kv, HD)
    scores = jnp.einsum('rkgd,rkld->rkgl', grouped, cache_keys.astype(jnp.float32)) * HD ** (-0.5)
    visible = lax.broadcasted_iota(jnp.int32, (REQ, SPAN), 1) < lengths[:, None]
    scores = jnp.where(visible[:, None, None, :], scores, -1e+30)
    attn_probs = jax.nn.softmax(scores, axis=-1).astype(jnp.bfloat16)
    attended = jnp.einsum('rkgl,rkld->rkgd', attn_probs.astype(jnp.float32), cache_values.astype(jnp.float32))
    attended = attended.astype(jnp.bfloat16).reshape(REQ, QH * HD)
    residual = hidden.astype(jnp.float32) + jnp.dot(attended, out_proj, preferred_element_type=jnp.float32)
    inverse = lax.rsqrt(lax.optimization_barrier(jnp.mean(residual * residual, axis=-1, keepdims=True)) + EPSILON)
    normed = (residual * inverse * norm_gain).astype(jnp.bfloat16)
    low_rank = jnp.dot(normed, low_factor, preferred_element_type=jnp.float32).astype(jnp.bfloat16)
    gate_pair = route_gates(normed, router, experts)
    mixture = jnp.zeros((REQ, D), jnp.float32)
    for expert in range(EXPERTS):
        columns = slice(expert * FF, (expert + 1) * FF)
        output = expert_shard(normed, low_rank, gate_weight[:, columns], up_weight[:, columns], down_weight[columns, :], gate_low[:, columns], up_low[:, columns])
        route_share = lax.optimization_barrier(jnp.sum(gate_pair * (experts == expert).astype(jnp.float32), axis=-1))
        mixture = mixture + route_share[:, None] * output
    return ((residual + mixture).astype(jnp.bfloat16), mixture)
```

```python
import functools

import jax
import jax.numpy as jnp
from jax import lax
from jax.experimental import pallas as pl
from jax.experimental.pallas import tpu as pltpu
from jax.sharding import PartitionSpec as P

CAP = 6


EPSILON = 1e-05


def expert_shard(row_block, low_rank, gate_weight, up_weight, down_weight, gate_low, up_low):
    gate_sum = jnp.dot(row_block, gate_weight, preferred_element_type=jnp.float32) + jnp.dot(
        low_rank, gate_low, preferred_element_type=jnp.float32
    )
    up_sum = jnp.dot(row_block, up_weight, preferred_element_type=jnp.float32) + jnp.dot(
        low_rank, up_low, preferred_element_type=jnp.float32
    )
    inner_act = (jax.nn.silu(gate_sum) * up_sum).astype(jnp.bfloat16)
    return jnp.dot(inner_act, down_weight, preferred_element_type=jnp.float32)


def route_gates(normed, router, experts):
    logits = jnp.dot(normed, router, preferred_element_type=jnp.float32)
    labels = lax.broadcasted_iota(jnp.int32, (1, 1, router.shape[1]), 2)
    picked = (experts[:, :, None] == labels).astype(jnp.float32)
    chosen = jnp.sum(logits[:, None, :] * picked, axis=-1)
    leading = jax.nn.sigmoid(chosen[:, 0] - chosen[:, 1])
    return jnp.stack([leading, 1.0 - leading], axis=-1)


def plain_body(
    hidden,
    query,
    cache_keys,
    cache_values,
    lengths,
    out_proj,
    norm_gain,
    router,
    low_factor,
    gate_weight,
    up_weight,
    down_weight,
    gate_low,
    up_low,
    experts,
):
    requests = hidden.shape[0]
    model_width = hidden.shape[1]
    heads_here = query.shape[1]
    kv_here = cache_keys.shape[1]
    span_len = cache_keys.shape[2]
    head_size = query.shape[2]
    grouped = query.reshape(requests, kv_here, heads_here // kv_here, head_size)
    scores = jnp.einsum(
        "rkgd,rkld->rkgl", grouped, cache_keys, preferred_element_type=jnp.float32
    ) * head_size ** (-0.5)
    visible = lax.broadcasted_iota(jnp.int32, (requests, span_len), 1) < lengths[:, None]
    scores = jnp.where(visible[:, None, None, :], scores, -1e30)
    attn_probs = jax.nn.softmax(scores, axis=-1).astype(jnp.bfloat16)
    attended = jnp.einsum(
        "rkgl,rkld->rkgd", attn_probs, cache_values, preferred_element_type=jnp.float32
    )
    attended = attended.astype(jnp.bfloat16).reshape(requests, heads_here * head_size)
    columns = jnp.dot(
        lax.all_gather(attended, "dev", axis=0, tiled=True),
        out_proj,
        preferred_element_type=jnp.float32,
    )
    partial_proj = lax.all_to_all(columns, "dev", split_axis=0, concat_axis=1, tiled=True)
    residual = hidden.astype(jnp.float32) + lax.psum(partial_proj, "sub")
    inverse = lax.rsqrt(jnp.mean(residual * residual, axis=-1, keepdims=True) + EPSILON)
    normed = (residual * inverse * norm_gain).astype(jnp.bfloat16)
    half_width = low_factor.shape[0]
    normed_half = lax.dynamic_slice_in_dim(
        normed, lax.axis_index("sub") * half_width, half_width, 1
    )
    low_partial = jnp.dot(normed_half, low_factor, preferred_element_type=jnp.float32)
    low_rank = lax.psum(low_partial, "sub").astype(jnp.bfloat16)
    rank_width = low_rank.shape[1]
    expert_count = router.shape[1]
    holders = lax.axis_size("dev") // expert_count
    gate_pair = route_gates(normed, router, experts)
    flat_ids = experts.reshape(-1)
    entries = flat_ids.shape[0]
    same_expert = flat_ids[:, None] == flat_ids[None, :]
    earlier = lax.broadcasted_iota(jnp.int32, (entries, entries), 0) > lax.broadcasted_iota(
        jnp.int32, (entries, entries), 1
    )
    slot_index = jnp.sum((same_expert & earlier).astype(jnp.int32), axis=1).reshape(requests, 2)
    target = experts * CAP + slot_index
    placement = (
        target[:, :, None] == lax.broadcasted_iota(jnp.int32, (1, 1, expert_count * CAP), 2)
    ).astype(jnp.float32)
    chosen = jnp.sum(placement, axis=1).astype(jnp.bfloat16)
    packed_rows = jnp.einsum(
        "rs,rd->sd", chosen, normed, preferred_element_type=jnp.float32
    ).astype(jnp.bfloat16)
    packed_low = jnp.einsum(
        "rs,rd->sd", chosen, low_rank, preferred_element_type=jnp.float32
    ).astype(jnp.bfloat16)
    send_rows = jnp.repeat(packed_rows.reshape(expert_count, CAP, model_width), holders, axis=0)
    send_low = jnp.repeat(packed_low.reshape(expert_count, CAP, rank_width), holders, axis=0)
    got_rows = lax.all_to_all(send_rows, "dev", split_axis=0, concat_axis=0, tiled=True)
    got_low = lax.all_to_all(send_low, "dev", split_axis=0, concat_axis=0, tiled=True)
    sources = got_rows.shape[0]
    slot_count = got_rows.shape[1]
    result = expert_shard(
        got_rows.reshape(sources * slot_count, model_width),
        got_low.reshape(sources * slot_count, rank_width),
        gate_weight,
        up_weight,
        down_weight,
        gate_low,
        up_low,
    )
    partials = result.reshape(sources, slot_count, model_width)
    returned = lax.all_to_all(
        partials.astype(jnp.bfloat16), "dev", split_axis=0, concat_axis=0, tiled=True
    ).astype(partials.dtype)
    per_slot = jnp.sum(returned.reshape(expert_count, holders, CAP, model_width), axis=1).reshape(
        expert_count * CAP, model_width
    )
    weighted = jnp.sum(placement * gate_pair[:, :, None], axis=1)
    mixture_part = jnp.dot(weighted, per_slot, precision=lax.Precision.HIGHEST)
    mixture = lax.psum(mixture_part.astype(jnp.bfloat16), "sub").astype(jnp.float32)
    return ((residual + mixture).astype(jnp.bfloat16), mixture)


CHUNK = 512
RING_BYTES = 42 * 2**20
VMEM_BYTES = 66 * 10**6
F32 = jnp.float32
BF16 = jnp.bfloat16


def layer_kernel(
    devs,
    subs,
    slots,
    hidden,
    query,
    keys,
    values,
    lengths,
    out_proj,
    gain,
    router,
    low_factor,
    gate_w,
    up_w,
    down_w,
    gate_low,
    up_low,
    experts,
    layer_out,
    mixture,
    ring,
    hid_v,
    q_v,
    k_v,
    v_v,
    op_v,
    lf_v,
    gl_v,
    ul_v,
    att_h,
    att_all,
    hid_all,
    exp_all,
    pair_send,
    pair_recv,
    res_all,
    res32,
    normed,
    low_send,
    low_recv,
    inner,
    dsend,
    drecv,
    rsend,
    rrecv,
    ring_sem,
    load_sem,
    bsend_sem,
    brecv_sem,
    csend_sem,
    crecv_sem,
    asend_sem,
    arecv_sem,
    gsend_sem,
    grecv_sem,
    fsend_sem,
    frecv_sem,
    psend_sem,
    precv_sem,
    xsend_sem,
    xrecv_sem,
    rs_sem,
    rr_sem,
    msend_sem,
    mrecv_sem,
):
    me = lax.axis_index("dev")
    s = lax.axis_index("sub")
    mate = 1 - s
    rows, width = hidden.shape
    all_rows = devs * rows
    heads = query.shape[1]
    kv_here, span, hd = keys.shape[1:]
    per_kv = heads // kv_here
    cols = out_proj.shape[1]
    part = cols // subs
    units = gate_w.shape[1]
    depth_blocks = width // units
    unit_blocks = units // CHUNK
    per_block = 2 * depth_blocks
    first_down = unit_blocks * per_block
    down_steps = width // (2 * CHUNK)
    total = first_down + 2 * down_steps
    blocks = devs * subs

    def peer(k):
        return lax.rem(me + k, devs)

    def remote(src, dst, send_sem, recv_sem, d, sub):
        return pltpu.make_async_remote_copy(
            src_ref=src,
            dst_ref=dst,
            send_sem=send_sem,
            recv_sem=recv_sem,
            device_id={"dev": d, "sub": sub},
            device_id_type=pl.DeviceIdType.MESH,
        )

    barrier = pltpu.get_barrier_semaphore()
    for k in range(1, devs):
        pl.semaphore_signal(
            barrier, inc=1, device_id={"dev": peer(k), "sub": s}, device_id_type=pl.DeviceIdType.MESH
        )
    pl.semaphore_signal(
        barrier, inc=1, device_id={"dev": me, "sub": mate}, device_id_type=pl.DeviceIdType.MESH
    )

    loads = [
        pltpu.make_async_copy(src, dst, load_sem.at[n])
        for n, (src, dst) in enumerate(
            [
                (query, q_v),
                (keys, k_v),
                (values, v_v),
                (hidden, hid_v),
                (out_proj, op_v),
                (low_factor, lf_v),
                (gate_low, gl_v),
                (up_low, ul_v),
            ]
        )
    ]
    for load in loads:
        load.start()

    def chunk_from(src, row, col, slot):
        return pltpu.make_async_copy(
            src.at[pl.ds(row, units), pl.ds(col, CHUNK)], ring.at[slot], ring_sem.at[slot]
        )

    def down_col(c):
        pair = c // 2
        return pl.multiple_of((2 * pair + jnp.where(c % 2 == 0, mate, s)) * CHUNK, CHUNK)

    def start_static(i):
        slot = i % slots
        if i < first_down:
            n, j = divmod(i, per_block)
            src = gate_w if j < depth_blocks else up_w
            chunk_from(src, (j % depth_blocks) * units, n * CHUNK, slot).start()
        else:
            chunk_from(down_w, 0, down_col(i - first_down), slot).start()

    for i in range(min(slots, total)):
        start_static(i)

    def refill(i):
        nxt = i + slots
        slot = lax.rem(nxt, slots)
        n = nxt // per_block
        j = lax.rem(nxt, per_block)
        col = pl.multiple_of(n * CHUNK, CHUNK)

        @pl.when((nxt < first_down) & (j < depth_blocks))
        def _():
            chunk_from(gate_w, pl.multiple_of(j * units, units), col, slot).start()

        @pl.when((nxt < first_down) & (j >= depth_blocks))
        def _():
            chunk_from(up_w, pl.multiple_of((j - depth_blocks) * units, units), col, slot).start()

        @pl.when((nxt >= first_down) & (nxt < total))
        def _():
            chunk_from(down_w, 0, down_col(nxt - first_down), slot).start()

    def await_chunk(i):
        slot = lax.rem(i, slots)
        chunk_from(gate_w, 0, 0, slot).wait()
        return slot

    lane = lax.broadcasted_iota(jnp.int32, (rows, 128), 1)
    exp_all[me] = jnp.where(lane == 0, experts[:, 0:1], experts[:, 1:2])
    loads[3].wait()
    mine = pl.multiple_of(me * cols + s * part, 128)
    hid_all[me] = hid_v[:, pl.ds(mine, part)]
    pl.semaphore_wait(barrier, devs)
    small = []
    for k in range(1, devs):
        p = peer(k)
        theirs = pl.multiple_of(p * cols + s * part, 128)
        small.append(
            remote(exp_all.at[me], exp_all.at[me], bsend_sem.at[k], brecv_sem.at[me], p, s)
        )
        small.append(
            remote(
                hid_v.at[:, pl.ds(theirs, part)],
                hid_all.at[me],
                csend_sem.at[k],
                crecv_sem.at[me],
                p,
                s,
            )
        )
    for copy in small:
        copy.start()

    for load in loads[:3]:
        load.wait()
    at = lax.broadcasted_iota(jnp.int32, (heads, kv_here * span), 1)
    head = lax.broadcasted_iota(jnp.int32, (heads, kv_here * span), 0)
    own = (at // span) == (head // per_kv)
    position = at % span
    for r in range(rows):
        scores = (
            lax.dot_general(
                q_v[r],
                k_v[r].reshape(kv_here * span, hd),
                (((1,), (1,)), ((), ())),
                preferred_element_type=F32,
            )
            * hd ** (-0.5)
        )
        scores = jnp.where(own & (position < lengths[r]), scores, -1e30)
        top = jnp.max(scores, axis=-1, keepdims=True)
        e = jnp.exp(scores - top)
        probs = (e / jnp.sum(e, axis=-1, keepdims=True)).astype(BF16)
        att_h[:, r, :] = jnp.dot(
            probs, v_v[r].reshape(kv_here * span, hd), preferred_element_type=F32
        )
    for h in range(heads):
        att_all[me, :, h * hd : (h + 1) * hd] = att_h[h].astype(BF16)

    def all_devs(src, dst, send_sem, recv_sem):
        out = []
        for k in range(1, devs):
            copy = remote(src, dst, send_sem.at[k], recv_sem.at[me], peer(k), s)
            copy.start()
            out.append(copy)
        return out

    att_sends = all_devs(att_all.at[me], att_all.at[me], asend_sem, arecv_sem)
    loads[4].wait()
    for k in range(1, devs):
        p = peer(k)
        remote(att_all.at[p], att_all.at[p], asend_sem.at[k], arecv_sem.at[p], p, s).wait_recv()
    attended = jnp.concatenate([att_all[d].astype(F32) for d in range(devs)], axis=0).astype(BF16)

    theirs = pl.multiple_of(mate * part, 128)
    pair_send[...] = jnp.dot(
        attended, op_v[:, pl.ds(theirs, part)], preferred_element_type=F32
    )
    pair_copy = remote(pair_send, pair_recv, psend_sem.at[0], precv_sem.at[0], me, mate)
    pair_copy.start()
    ours = pl.multiple_of(s * part, 128)
    projected = jnp.dot(attended, op_v[:, pl.ds(ours, part)], preferred_element_type=F32)
    for k in range(1, devs):
        p = peer(k)
        remote(exp_all.at[p], exp_all.at[p], bsend_sem.at[k], brecv_sem.at[p], p, s).wait_recv()
        remote(
            hid_all.at[p], hid_all.at[p], csend_sem.at[k], crecv_sem.at[p], p, s
        ).wait_recv()
    own_hidden = jnp.concatenate([hid_all[d].astype(F32) for d in range(devs)], axis=0)
    pair_copy.wait_recv()
    my_block = me * subs + s
    res_all[my_block] = (own_hidden + (projected + pair_recv[...])).astype(BF16)

    res_sends = []
    copy = remote(
        res_all.at[my_block],
        res_all.at[my_block],
        fsend_sem.at[0],
        frecv_sem.at[me],
        me,
        mate,
    )
    for k in range(1, devs):
        c = remote(
            res_all.at[my_block],
            res_all.at[my_block],
            gsend_sem.at[k],
            grecv_sem.at[me],
            peer(k),
            s,
        )
        c.start()
        res_sends.append(c)
    copy.start()
    res_sends.append(copy)
    for k in range(1, devs):
        p = peer(k)
        b = p * subs + s
        remote(res_all.at[b], res_all.at[b], gsend_sem.at[k], grecv_sem.at[p], p, s).wait_recv()
        c = remote(res_all.at[b], res_all.at[b], fsend_sem.at[k], frecv_sem.at[p], me, mate)
        c.start()
        res_sends.append(c)
    for k in range(devs):
        p = peer(k)
        b = p * subs + mate
        remote(res_all.at[b], res_all.at[b], fsend_sem.at[k], frecv_sem.at[p], me, mate).wait_recv()

    squares = jnp.zeros((all_rows, 1), F32)
    for b in range(blocks):
        x = res_all[b].astype(F32)
        res32[:, b * part : (b + 1) * part] = x
        squares = squares + jnp.sum(x * x, axis=-1, keepdims=True)
    inverse = lax.rsqrt(squares / width + EPSILON)
    for b in range(blocks):
        at_cols = slice(b * part, (b + 1) * part)
        normed[:, at_cols] = (res32[:, at_cols] * inverse * gain[:, at_cols]).astype(BF16)

    half = low_factor.shape[0]
    loads[5].wait()
    low_send[...] = jnp.dot(
        normed[:, pl.ds(pl.multiple_of(s * half, 128), half)], lf_v[...], preferred_element_type=F32
    )
    low_copy = remote(low_send, low_recv, psend_sem.at[1], precv_sem.at[1], me, mate)
    low_copy.start()

    logits = lax.dot_general(
        normed[...], router[...], (((1,), (1,)), ((), ())), preferred_element_type=F32
    )
    count = router.shape[0]
    label = lax.broadcasted_iota(jnp.int32, (all_rows, count), 1)
    named = exp_all[...].reshape(all_rows, 128)
    e0 = named[:, 0:1]
    e1 = named[:, 1:2]
    a = jnp.sum(jnp.where(label == e0, logits, 0.0), axis=-1, keepdims=True)
    b = jnp.sum(jnp.where(label == e1, logits, 0.0), axis=-1, keepdims=True)
    lead = jax.nn.sigmoid(a - b)
    here = me // (devs // count)
    share = jnp.where(e0 == here, lead, 0.0) + jnp.where(e1 == here, 1.0 - lead, 0.0)

    loads[6].wait()
    loads[7].wait()
    low_copy.wait_recv()
    low = (low_send[...] + low_recv[...]).astype(BF16)

    def unit_step(n, carry):
        at_units = pl.ds(pl.multiple_of(n * CHUNK, CHUNK), CHUNK)
        gate_sum = jnp.dot(low, gl_v[:, at_units], preferred_element_type=F32)
        up_sum = jnp.dot(low, ul_v[:, at_units], preferred_element_type=F32)
        for j in range(depth_blocks):
            i = n * per_block + j
            slot = await_chunk(i)
            gate_sum += jnp.dot(
                normed[:, j * units : (j + 1) * units], ring[slot], preferred_element_type=F32
            )
            refill(i)
        for j in range(depth_blocks):
            i = n * per_block + depth_blocks + j
            slot = await_chunk(i)
            up_sum += jnp.dot(
                normed[:, j * units : (j + 1) * units], ring[slot], preferred_element_type=F32
            )
            refill(i)
        inner[:, at_units] = (gate_sum / (1.0 + jnp.exp(-gate_sum)) * up_sum).astype(BF16)
        return carry

    lax.fori_loop(0, unit_blocks, unit_step, 0)

    def down_step(c, carry):
        i = first_down + 2 * c
        slot = await_chunk(i)
        dsend[c] = (
            jnp.dot(inner[...], ring[slot], preferred_element_type=F32) * share
        ).astype(BF16)
        remote(dsend.at[c], drecv.at[c], xsend_sem.at[c], xrecv_sem.at[c], me, mate).start()
        refill(i)
        slot = await_chunk(i + 1)
        y = jnp.dot(inner[...], ring[slot], preferred_element_type=F32) * share
        refill(i + 1)
        remote(dsend.at[c], drecv.at[c], xsend_sem.at[c], xrecv_sem.at[c], me, mate).wait_recv()
        y = y + drecv[c].astype(F32)
        for d in range(devs):
            rsend[c, d] = y[d * rows : (d + 1) * rows].astype(BF16)
        rrecv[c, me] = rsend[c, me]
        for k in range(1, devs):
            p = peer(k)
            remote(
                rsend.at[c, p], rrecv.at[c, me], rs_sem.at[c, k], rr_sem.at[c, me], p, s
            ).start()
        return carry

    lax.fori_loop(0, down_steps, down_step, 0)

    def sum_step(c, carry):
        for k in range(1, devs):
            p = peer(k)
            remote(
                rsend.at[c, p], rrecv.at[c, p], rs_sem.at[c, k], rr_sem.at[c, p], p, s
            ).wait_recv()
        got = rrecv[c, 0].astype(F32)
        for d in range(1, devs):
            got = got + rrecv[c, d].astype(F32)
        at_cols = pl.ds(pl.multiple_of((2 * c + s) * CHUNK, CHUNK), CHUNK)
        mixture[:, at_cols] = got
        remote(
            mixture.at[:, at_cols],
            mixture.at[:, at_cols],
            msend_sem.at[c],
            mrecv_sem.at[c],
            me,
            mate,
        ).start()
        return carry

    lax.fori_loop(0, down_steps, sum_step, 0)

    def last_step(c, carry):
        at_cols = pl.ds(pl.multiple_of((2 * c + mate) * CHUNK, CHUNK), CHUNK)
        swap = remote(
            mixture.at[:, at_cols],
            mixture.at[:, at_cols],
            msend_sem.at[c],
            mrecv_sem.at[c],
            me,
            mate,
        )
        swap.wait()
        remote(dsend.at[c], drecv.at[c], xsend_sem.at[c], xrecv_sem.at[c], me, mate).wait_send()
        for k in range(1, devs):
            p = peer(k)
            remote(
                rsend.at[c, p], rrecv.at[c, me], rs_sem.at[c, k], rr_sem.at[c, me], p, s
            ).wait_send()
        return carry

    lax.fori_loop(0, down_steps, last_step, 0)
    my_rows = pl.ds(pl.multiple_of(me * rows, rows), rows)
    layer_out[...] = (res32[my_rows, :] + mixture[...]).astype(BF16)
    for copy in small + att_sends + res_sends + [pair_copy, low_copy]:
        copy.wait_send()


def fits(mesh, shapes):
    devs, subs = mesh.shape["dev"], mesh.shape["sub"]
    hidden, query, keys, out_proj, router, gate_w = shapes
    width = hidden[1]
    units = gate_w[1]
    return (
        subs == 2
        and devs * hidden[0] <= 128
        and hidden[0] == 8
        and query[2] == 128
        and out_proj[1] % (128 * subs) == 0
        and units % CHUNK == 0
        and width % units == 0
        and width % (2 * CHUNK) == 0
        and devs % router[1] == 0
    )


def body(mesh, *args):
    (
        hidden,
        query,
        keys,
        values,
        lengths,
        out_proj,
        gain,
        router,
        low_factor,
        gate_w,
        up_w,
        down_w,
        gate_low,
        up_low,
        experts,
    ) = args
    shapes = [x.shape for x in (hidden, query, keys, out_proj, router, gate_w)]
    if not fits(mesh, shapes):
        return plain_body(*args)
    devs, subs = mesh.shape["dev"], mesh.shape["sub"]
    rows, width = hidden.shape
    all_rows = devs * rows
    heads, hd = query.shape[1:]
    part = out_proj.shape[1] // subs
    units = gate_w.shape[1]
    rank = low_factor.shape[1]
    down_steps = width // (2 * CHUNK)
    total = 2 * (width // units) * (units // CHUNK) + 2 * down_steps
    slots = min(total, RING_BYTES // (units * CHUNK * 2))
    anywhere = pl.BlockSpec(memory_space=pl.ANY)
    vmem = pl.BlockSpec(memory_space=pltpu.VMEM)
    smem = pl.BlockSpec(memory_space=pltpu.SMEM)
    dma = pltpu.SemaphoreType.DMA
    scratch = [
        pltpu.VMEM((slots, units, CHUNK), BF16),
        pltpu.VMEM(hidden.shape, BF16),
        pltpu.VMEM(query.shape, BF16),
        pltpu.VMEM(keys.shape, BF16),
        pltpu.VMEM(values.shape, BF16),
        pltpu.VMEM(out_proj.shape, BF16),
        pltpu.VMEM(low_factor.shape, BF16),
        pltpu.VMEM(gate_low.shape, BF16),
        pltpu.VMEM(up_low.shape, BF16),
        pltpu.VMEM((heads, rows, hd), F32),
        pltpu.VMEM((devs, rows, heads * hd), BF16),
        pltpu.VMEM((devs, rows, part), BF16),
        pltpu.VMEM((devs, rows, 128), jnp.int32),
        pltpu.VMEM((all_rows, part), F32),
        pltpu.VMEM((all_rows, part), F32),
        pltpu.VMEM((devs * subs, all_rows, part), BF16),
        pltpu.VMEM((all_rows, width), F32),
        pltpu.VMEM((all_rows, width), BF16),
        pltpu.VMEM((all_rows, rank), F32),
        pltpu.VMEM((all_rows, rank), F32),
        pltpu.VMEM((all_rows, units), BF16),
        pltpu.VMEM((down_steps, all_rows, CHUNK), BF16),
        pltpu.VMEM((down_steps, all_rows, CHUNK), BF16),
        pltpu.VMEM((down_steps, devs, rows, CHUNK), BF16),
        pltpu.VMEM((down_steps, devs, rows, CHUNK), BF16),
        dma((slots,)),
        dma((8,)),
    ]
    scratch += [dma((devs,)) for _ in range(10)]
    scratch += [dma((2,)), dma((2,)), dma((down_steps,)), dma((down_steps,))]
    scratch += [dma((down_steps, devs)), dma((down_steps, devs))]
    scratch += [dma((down_steps,)), dma((down_steps,))]
    return pl.pallas_call(
        functools.partial(layer_kernel, devs, subs, slots),
        out_shape=(
            jax.ShapeDtypeStruct((rows, width), BF16),
            jax.ShapeDtypeStruct((rows, width), F32),
        ),
        in_specs=[anywhere] * 4
        + [smem, anywhere, vmem, vmem]
        + [anywhere] * 6
        + [vmem],
        out_specs=(vmem, vmem),
        scratch_shapes=scratch,
        compiler_params=pltpu.CompilerParams(
            collective_id=0, has_side_effects=True, vmem_limit_bytes=VMEM_BYTES
        ),
    )(
        hidden,
        query,
        keys,
        values,
        lengths,
        out_proj,
        gain.reshape(1, width),
        router.T,
        low_factor,
        gate_w,
        up_w,
        down_w,
        gate_low,
        up_low,
        experts,
    )


def solution(mesh):
    placed = (
        P(("groups", "dev"), None),
        P(("groups", "dev"), "sub", None),
        P(("groups", "dev"), "sub", None, None),
        P(("groups", "dev"), "sub", None, None),
        P(("groups", "dev")),
        P("sub", "dev"),
        P(),
        P(),
        P("sub", None),
        P(None, ("dev", "sub")),
        P(None, ("dev", "sub")),
        P(("dev", "sub"), None),
        P(None, ("dev", "sub")),
        P(None, ("dev", "sub")),
        P(("groups", "dev"), None),
    )
    return jax.shard_map(
        functools.partial(body, mesh),
        mesh=mesh,
        in_specs=placed,
        out_specs=(P(("groups", "dev"), None), P(("groups", "dev"), None)),
        check_vma=False,
    )
```

```python
import functools

import jax
import jax.numpy as jnp
from jax import lax
from jax.experimental import pallas as pl
from jax.experimental.pallas import tpu as pltpu
from jax.sharding import PartitionSpec as P

CAP = 6


EPSILON = 1e-05


def expert_shard(row_block, low_rank, gate_weight, up_weight, down_weight, gate_low, up_low):
    gate_sum = jnp.dot(row_block, gate_weight, preferred_element_type=jnp.float32) + jnp.dot(
        low_rank, gate_low, preferred_element_type=jnp.float32
    )
    up_sum = jnp.dot(row_block, up_weight, preferred_element_type=jnp.float32) + jnp.dot(
        low_rank, up_low, preferred_element_type=jnp.float32
    )
    inner_act = (jax.nn.silu(gate_sum) * up_sum).astype(jnp.bfloat16)
    return jnp.dot(inner_act, down_weight, preferred_element_type=jnp.float32)


def route_gates(normed, router, experts):
    logits = jnp.dot(normed, router, preferred_element_type=jnp.float32)
    labels = lax.broadcasted_iota(jnp.int32, (1, 1, router.shape[1]), 2)
    picked = (experts[:, :, None] == labels).astype(jnp.float32)
    chosen = jnp.sum(logits[:, None, :] * picked, axis=-1)
    leading = jax.nn.sigmoid(chosen[:, 0] - chosen[:, 1])
    return jnp.stack([leading, 1.0 - leading], axis=-1)


def plain_body(
    hidden,
    query,
    cache_keys,
    cache_values,
    lengths,
    out_proj,
    norm_gain,
    router,
    low_factor,
    gate_weight,
    up_weight,
    down_weight,
    gate_low,
    up_low,
    experts,
):
    requests = hidden.shape[0]
    model_width = hidden.shape[1]
    heads_here = query.shape[1]
    kv_here = cache_keys.shape[1]
    span_len = cache_keys.shape[2]
    head_size = query.shape[2]
    grouped = query.reshape(requests, kv_here, heads_here // kv_here, head_size)
    scores = jnp.einsum(
        "rkgd,rkld->rkgl", grouped, cache_keys, preferred_element_type=jnp.float32
    ) * head_size ** (-0.5)
    visible = lax.broadcasted_iota(jnp.int32, (requests, span_len), 1) < lengths[:, None]
    scores = jnp.where(visible[:, None, None, :], scores, -1e30)
    attn_probs = jax.nn.softmax(scores, axis=-1).astype(jnp.bfloat16)
    attended = jnp.einsum(
        "rkgl,rkld->rkgd", attn_probs, cache_values, preferred_element_type=jnp.float32
    )
    attended = attended.astype(jnp.bfloat16).reshape(requests, heads_here * head_size)
    columns = jnp.dot(
        lax.all_gather(attended, "dev", axis=0, tiled=True),
        out_proj,
        preferred_element_type=jnp.float32,
    )
    partial_proj = lax.all_to_all(columns, "dev", split_axis=0, concat_axis=1, tiled=True)
    residual = hidden.astype(jnp.float32) + lax.psum(partial_proj, "sub")
    inverse = lax.rsqrt(jnp.mean(residual * residual, axis=-1, keepdims=True) + EPSILON)
    normed = (residual * inverse * norm_gain).astype(jnp.bfloat16)
    half_width = low_factor.shape[0]
    normed_half = lax.dynamic_slice_in_dim(
        normed, lax.axis_index("sub") * half_width, half_width, 1
    )
    low_partial = jnp.dot(normed_half, low_factor, preferred_element_type=jnp.float32)
    low_rank = lax.psum(low_partial, "sub").astype(jnp.bfloat16)
    rank_width = low_rank.shape[1]
    expert_count = router.shape[1]
    holders = lax.axis_size("dev") // expert_count
    gate_pair = route_gates(normed, router, experts)
    flat_ids = experts.reshape(-1)
    entries = flat_ids.shape[0]
    same_expert = flat_ids[:, None] == flat_ids[None, :]
    earlier = lax.broadcasted_iota(jnp.int32, (entries, entries), 0) > lax.broadcasted_iota(
        jnp.int32, (entries, entries), 1
    )
    slot_index = jnp.sum((same_expert & earlier).astype(jnp.int32), axis=1).reshape(requests, 2)
    target = experts * CAP + slot_index
    placement = (
        target[:, :, None] == lax.broadcasted_iota(jnp.int32, (1, 1, expert_count * CAP), 2)
    ).astype(jnp.float32)
    chosen = jnp.sum(placement, axis=1).astype(jnp.bfloat16)
    packed_rows = jnp.einsum(
        "rs,rd->sd", chosen, normed, preferred_element_type=jnp.float32
    ).astype(jnp.bfloat16)
    packed_low = jnp.einsum(
        "rs,rd->sd", chosen, low_rank, preferred_element_type=jnp.float32
    ).astype(jnp.bfloat16)
    send_rows = jnp.repeat(packed_rows.reshape(expert_count, CAP, model_width), holders, axis=0)
    send_low = jnp.repeat(packed_low.reshape(expert_count, CAP, rank_width), holders, axis=0)
    got_rows = lax.all_to_all(send_rows, "dev", split_axis=0, concat_axis=0, tiled=True)
    got_low = lax.all_to_all(send_low, "dev", split_axis=0, concat_axis=0, tiled=True)
    sources = got_rows.shape[0]
    slot_count = got_rows.shape[1]
    result = expert_shard(
        got_rows.reshape(sources * slot_count, model_width),
        got_low.reshape(sources * slot_count, rank_width),
        gate_weight,
        up_weight,
        down_weight,
        gate_low,
        up_low,
    )
    partials = result.reshape(sources, slot_count, model_width)
    returned = lax.all_to_all(
        partials.astype(jnp.bfloat16), "dev", split_axis=0, concat_axis=0, tiled=True
    ).astype(partials.dtype)
    per_slot = jnp.sum(returned.reshape(expert_count, holders, CAP, model_width), axis=1).reshape(
        expert_count * CAP, model_width
    )
    weighted = jnp.sum(placement * gate_pair[:, :, None], axis=1)
    mixture_part = jnp.dot(weighted, per_slot, precision=lax.Precision.HIGHEST)
    mixture = lax.psum(mixture_part.astype(jnp.bfloat16), "sub").astype(jnp.float32)
    return ((residual + mixture).astype(jnp.bfloat16), mixture)


CHUNK = 512
NEAR = 2
RING_BYTES = 42 * 2**20
VMEM_BYTES = 66 * 10**6
STAGES = (0, 8, 16)
F32 = jnp.float32
BF16 = jnp.bfloat16


def layer_kernel(
    devs,
    subs,
    slots,
    hidden,
    query,
    keys,
    values,
    lengths,
    out_proj,
    gain,
    router,
    low_factor,
    gate_w,
    up_w,
    down_w,
    gate_low,
    up_low,
    experts,
    residual,
    mixture,
    ring,
    hid_v,
    q_v,
    k_v,
    v_v,
    op_v,
    lf_v,
    gl_v,
    ul_v,
    att_h,
    att_all,
    hid_all,
    exp_all,
    pair_send,
    pair_recv,
    res_all,
    res32,
    normed,
    low_send,
    low_recv,
    inner,
    kept,
    dsend,
    drecv,
    rsend,
    rrecv,
    ring_sem,
    load_sem,
    bsend_sem,
    brecv_sem,
    csend_sem,
    crecv_sem,
    asend_sem,
    arecv_sem,
    gsend_sem,
    grecv_sem,
    fsend_sem,
    frecv_sem,
    psend_sem,
    precv_sem,
    xsend_sem,
    xrecv_sem,
    rs_sem,
    rr_sem,
    msend_sem,
    mrecv_sem,
):
    me = lax.axis_index("dev")
    s = lax.axis_index("sub")
    mate = 1 - s
    rows, width = hidden.shape
    all_rows = devs * rows
    heads = query.shape[1]
    kv_here, span, hd = keys.shape[1:]
    per_kv = heads // kv_here
    cols = out_proj.shape[1]
    part = cols // subs
    units = gate_w.shape[1]
    depth_blocks = width // units
    unit_blocks = units // CHUNK
    per_block = 2 * depth_blocks
    first_down = unit_blocks * per_block
    down_steps = width // (2 * CHUNK)
    total = first_down + 2 * down_steps
    blocks = devs * subs

    def peer(k):
        return lax.rem(me + k, devs)

    def remote(src, dst, send_sem, recv_sem, d, sub):
        return pltpu.make_async_remote_copy(
            src_ref=src,
            dst_ref=dst,
            send_sem=send_sem,
            recv_sem=recv_sem,
            device_id={"dev": d, "sub": sub},
            device_id_type=pl.DeviceIdType.MESH,
        )

    barrier = pltpu.get_barrier_semaphore()
    for k in range(1, devs):
        pl.semaphore_signal(
            barrier, inc=1, device_id={"dev": peer(k), "sub": s}, device_id_type=pl.DeviceIdType.MESH
        )
    pl.semaphore_signal(
        barrier, inc=1, device_id={"dev": me, "sub": mate}, device_id_type=pl.DeviceIdType.MESH
    )

    loads = [
        pltpu.make_async_copy(src, dst, load_sem.at[n])
        for n, (src, dst) in enumerate(
            [
                (query, q_v),
                (keys, k_v),
                (values, v_v),
                (hidden, hid_v),
                (out_proj, op_v),
                (low_factor, lf_v),
                (gate_low, gl_v),
                (up_low, ul_v),
            ]
        )
    ]
    for load in loads:
        load.start()

    def chunk_from(src, row, col, slot):
        return pltpu.make_async_copy(
            src.at[pl.ds(row, units), pl.ds(col, CHUNK)], ring.at[slot], ring_sem.at[slot]
        )

    def down_col(c):
        pair = c // 2
        return pl.multiple_of((2 * pair + jnp.where(c % 2 == 0, mate, s)) * CHUNK, CHUNK)

    def start_static(i):
        slot = i % slots
        if i < first_down:
            n, j = divmod(i, per_block)
            src = gate_w if j < depth_blocks else up_w
            chunk_from(src, (j % depth_blocks) * units, n * CHUNK, slot).start()
        else:
            chunk_from(down_w, 0, down_col(i - first_down), slot).start()

    def prefetch(stage):
        for i in range(slots):
            if sum(i >= edge * slots // 20 for edge in STAGES) == stage:
                start_static(i)

    prefetch(0)

    def refill(i):
        nxt = i + slots
        slot = lax.rem(nxt, slots)
        n = nxt // per_block
        j = lax.rem(nxt, per_block)
        col = pl.multiple_of(n * CHUNK, CHUNK)

        @pl.when((nxt < first_down) & (j < depth_blocks))
        def _():
            chunk_from(gate_w, pl.multiple_of(j * units, units), col, slot).start()

        @pl.when((nxt < first_down) & (j >= depth_blocks))
        def _():
            chunk_from(up_w, pl.multiple_of((j - depth_blocks) * units, units), col, slot).start()

        @pl.when((nxt >= first_down) & (nxt < total))
        def _():
            chunk_from(down_w, 0, down_col(nxt - first_down), slot).start()

    def await_chunk(i):
        slot = lax.rem(i, slots)
        chunk_from(gate_w, 0, 0, slot).wait()
        return slot

    lane = lax.broadcasted_iota(jnp.int32, (rows, 128), 1)
    row = lax.broadcasted_iota(jnp.int32, (rows, 128), 0)
    named = jnp.zeros((rows, 128), jnp.int32)
    for r in range(rows):
        named = jnp.where(row == r, jnp.where(lane == 0, experts[0, r], experts[1, r]), named)
    exp_all[me] = named
    loads[3].wait()
    mine = pl.multiple_of(me * cols + s * part, 128)
    hid_all[me] = hid_v[:, pl.ds(mine, part)]
    pl.semaphore_wait(barrier, devs)
    small = []
    for k in range(1, devs):
        p = peer(k)
        theirs = pl.multiple_of(p * cols + s * part, 128)
        small.append(
            remote(exp_all.at[me], exp_all.at[me], bsend_sem.at[k], brecv_sem.at[me], p, s)
        )
        small.append(
            remote(
                hid_v.at[:, pl.ds(theirs, part)],
                hid_all.at[me],
                csend_sem.at[k],
                crecv_sem.at[me],
                p,
                s,
            )
        )
    for copy in small:
        copy.start()

    for load in loads[:3]:
        load.wait()
    at = lax.broadcasted_iota(jnp.int32, (heads, kv_here * span), 1)
    head = lax.broadcasted_iota(jnp.int32, (heads, kv_here * span), 0)
    own = (at // span) == (head // per_kv)
    position = at % span
    for r in range(rows):
        scores = (
            lax.dot_general(
                q_v[r],
                k_v[r].reshape(kv_here * span, hd),
                (((1,), (1,)), ((), ())),
                preferred_element_type=F32,
            )
            * hd ** (-0.5)
        )
        scores = jnp.where(own & (position < lengths[r]), scores, -1e30)
        top = jnp.max(scores, axis=-1, keepdims=True)
        e = jnp.exp(scores - top)
        probs = (e / jnp.sum(e, axis=-1, keepdims=True)).astype(BF16)
        att_h[:, r, :] = jnp.dot(
            probs, v_v[r].reshape(kv_here * span, hd), preferred_element_type=F32
        )
    for h in range(heads):
        att_all[me, :, h * hd : (h + 1) * hd] = att_h[h].astype(BF16)

    far = devs // NEAR
    beside = me + 1 - 2 * lax.rem(me, NEAR)

    def far_peer(k):
        return lax.rem(me + NEAR * k, devs)

    def gather_start(buf, index, send_sem, recv_sem):
        block = buf.at[index(me)]
        out = []
        for k in range(1, far):
            out.append(remote(block, block, send_sem.at[k], recv_sem.at[me], far_peer(k), s))
        out.append(remote(block, block, send_sem.at[far], recv_sem.at[me], beside, s))
        for copy in out:
            copy.start()
        return out

    def gather_finish(buf, index, send_sem, recv_sem, out, arrived):
        for k in range(1, far):
            p = far_peer(k)
            block = buf.at[index(p)]
            remote(block, block, send_sem.at[k], recv_sem.at[p], p, s).wait_recv()
            copy = remote(block, block, send_sem.at[far + k], recv_sem.at[p], beside, s)
            copy.start()
            out.append(copy)
            arrived(p, k)
        for k in range(far):
            p = lax.rem(beside + NEAR * k, devs)
            block = buf.at[index(p)]
            remote(block, block, send_sem.at[far], recv_sem.at[p], beside, s).wait_recv()
            arrived(p, far + k)

    same = lambda p: p
    att_sends = gather_start(att_all, same, asend_sem, arecv_sem)
    prefetch(1)
    gather_finish(att_all, same, asend_sem, arecv_sem, att_sends, lambda p, k: None)
    loads[4].wait()
    attended = jnp.concatenate([att_all[d].astype(F32) for d in range(devs)], axis=0).astype(BF16)

    theirs = pl.multiple_of(mate * part, 128)
    pair_send[...] = jnp.dot(
        attended, op_v[:, pl.ds(theirs, part)], preferred_element_type=F32
    )
    pair_copy = remote(pair_send, pair_recv, psend_sem.at[0], precv_sem.at[0], me, mate)
    pair_copy.start()
    ours = pl.multiple_of(s * part, 128)
    projected = jnp.dot(attended, op_v[:, pl.ds(ours, part)], preferred_element_type=F32)
    for k in range(1, devs):
        p = peer(k)
        remote(exp_all.at[p], exp_all.at[p], bsend_sem.at[k], brecv_sem.at[p], p, s).wait_recv()
        remote(
            hid_all.at[p], hid_all.at[p], csend_sem.at[k], crecv_sem.at[p], p, s
        ).wait_recv()
    own_hidden = jnp.concatenate([hid_all[d].astype(F32) for d in range(devs)], axis=0)
    pair_copy.wait_recv()
    my_block = me * subs + s
    res_all[my_block] = (own_hidden + (projected + pair_recv[...])).astype(BF16)

    def block_of(p):
        return p * subs + s

    res_sends = gather_start(res_all, block_of, gsend_sem, grecv_sem)

    def over(p, k):
        block = res_all.at[block_of(p)]
        copy = remote(block, block, fsend_sem.at[k], frecv_sem.at[p], me, mate)
        copy.start()
        res_sends.append(copy)

    over(me, 0)
    prefetch(2)
    gather_finish(res_all, block_of, gsend_sem, grecv_sem, res_sends, over)
    for k in range(devs):
        p = peer(k)
        block = res_all.at[p * subs + mate]
        remote(block, block, fsend_sem.at[k], frecv_sem.at[p], me, mate).wait_recv()
    prefetch(3)

    squares = jnp.zeros((all_rows, 1), F32)
    for b in range(blocks):
        x = res_all[b].astype(F32)
        res32[:, b * part : (b + 1) * part] = x
        squares = squares + jnp.sum(x * x, axis=-1, keepdims=True)
    inverse = lax.rsqrt(squares / width + EPSILON)
    for b in range(blocks):
        at_cols = slice(b * part, (b + 1) * part)
        normed[:, at_cols] = (res32[:, at_cols] * inverse * gain[:, at_cols]).astype(BF16)

    half = low_factor.shape[0]
    loads[5].wait()
    low_send[...] = jnp.dot(
        normed[:, pl.ds(pl.multiple_of(s * half, 128), half)], lf_v[...], preferred_element_type=F32
    )
    low_copy = remote(low_send, low_recv, psend_sem.at[1], precv_sem.at[1], me, mate)
    low_copy.start()

    logits = lax.dot_general(
        normed[...], router[...], (((1,), (1,)), ((), ())), preferred_element_type=F32
    )
    count = router.shape[0]
    label = lax.broadcasted_iota(jnp.int32, (all_rows, count), 1)
    named = exp_all[...].reshape(all_rows, 128)
    e0 = named[:, 0:1]
    e1 = named[:, 1:2]
    a = jnp.sum(jnp.where(label == e0, logits, 0.0), axis=-1, keepdims=True)
    b = jnp.sum(jnp.where(label == e1, logits, 0.0), axis=-1, keepdims=True)
    lead = jax.nn.sigmoid(a - b)
    here = me // (devs // count)
    share = jnp.where(e0 == here, lead, 0.0) + jnp.where(e1 == here, 1.0 - lead, 0.0)

    loads[6].wait()
    loads[7].wait()
    low_copy.wait_recv()
    low = (low_send[...] + low_recv[...]).astype(BF16)

    def unit_step(n, carry):
        at_units = pl.ds(pl.multiple_of(n * CHUNK, CHUNK), CHUNK)
        gate_sum = jnp.dot(low, gl_v[:, at_units], preferred_element_type=F32)
        up_sum = jnp.dot(low, ul_v[:, at_units], preferred_element_type=F32)
        for j in range(depth_blocks):
            i = n * per_block + j
            slot = await_chunk(i)
            gate_sum += jnp.dot(
                normed[:, j * units : (j + 1) * units], ring[slot], preferred_element_type=F32
            )
            refill(i)
        for j in range(depth_blocks):
            i = n * per_block + depth_blocks + j
            slot = await_chunk(i)
            up_sum += jnp.dot(
                normed[:, j * units : (j + 1) * units], ring[slot], preferred_element_type=F32
            )
            refill(i)
        inner[:, at_units] = (gate_sum / (1.0 + jnp.exp(-gate_sum)) * up_sum).astype(BF16)
        return carry

    lax.fori_loop(0, unit_blocks, unit_step, 0)

    def give_back(c):
        remote(dsend.at[c], drecv.at[c], xsend_sem.at[c], xrecv_sem.at[c], me, mate).wait_recv()
        y = kept[c % 2] + drecv[c].astype(F32)
        for d in range(devs):
            rsend[c, d] = y[d * rows : (d + 1) * rows].astype(BF16)
        rrecv[c, me] = rsend[c, me]
        for k in range(1, devs):
            p = peer(k)
            remote(
                rsend.at[c, p], rrecv.at[c, me], rs_sem.at[c, k], rr_sem.at[c, me], p, s
            ).start()

    def down_step(c, carry):
        i = first_down + 2 * c
        slot = await_chunk(i)
        dsend[c] = (
            jnp.dot(inner[...], ring[slot], preferred_element_type=F32) * share
        ).astype(BF16)
        remote(dsend.at[c], drecv.at[c], xsend_sem.at[c], xrecv_sem.at[c], me, mate).start()
        refill(i)
        slot = await_chunk(i + 1)
        kept[lax.rem(c, 2)] = jnp.dot(inner[...], ring[slot], preferred_element_type=F32) * share
        refill(i + 1)

        @pl.when(c > 0)
        def _():
            give_back(c - 1)

        return carry

    lax.fori_loop(0, down_steps, down_step, 0)
    give_back(down_steps - 1)

    def sum_step(c, carry):
        for k in range(1, devs):
            p = peer(k)
            remote(
                rsend.at[c, p], rrecv.at[c, p], rs_sem.at[c, k], rr_sem.at[c, p], p, s
            ).wait_recv()
        got = rrecv[c, 0].astype(F32)
        for d in range(1, devs):
            got = got + rrecv[c, d].astype(F32)
        at_cols = pl.ds(pl.multiple_of((2 * c + s) * CHUNK, CHUNK), CHUNK)
        mixture[:, at_cols] = got
        remote(
            mixture.at[:, at_cols],
            mixture.at[:, at_cols],
            msend_sem.at[c],
            mrecv_sem.at[c],
            me,
            mate,
        ).start()
        return carry

    lax.fori_loop(0, down_steps, sum_step, 0)

    def last_step(c, carry):
        at_cols = pl.ds(pl.multiple_of((2 * c + mate) * CHUNK, CHUNK), CHUNK)
        swap = remote(
            mixture.at[:, at_cols],
            mixture.at[:, at_cols],
            msend_sem.at[c],
            mrecv_sem.at[c],
            me,
            mate,
        )
        swap.wait()
        remote(dsend.at[c], drecv.at[c], xsend_sem.at[c], xrecv_sem.at[c], me, mate).wait_send()
        for k in range(1, devs):
            p = peer(k)
            remote(
                rsend.at[c, p], rrecv.at[c, me], rs_sem.at[c, k], rr_sem.at[c, me], p, s
            ).wait_send()
        return carry

    lax.fori_loop(0, down_steps, last_step, 0)
    my_rows = pl.ds(pl.multiple_of(me * rows, rows), rows)
    residual[...] = res32[my_rows, :]
    for copy in small + att_sends + res_sends + [pair_copy, low_copy]:
        copy.wait_send()


def add_kernel(residual, mixture, layer_out, mixture_out):
    mixture_out[...] = mixture[...]
    layer_out[...] = (residual[...] + mixture[...]).astype(BF16)


def fits(mesh, shapes):
    devs, subs = mesh.shape["dev"], mesh.shape["sub"]
    hidden, query, keys, out_proj, router, gate_w = shapes
    width = hidden[1]
    units = gate_w[1]
    return (
        subs == 2
        and devs * hidden[0] <= 128
        and hidden[0] == 8
        and query[2] == 128
        and out_proj[1] % (128 * subs) == 0
        and units % CHUNK == 0
        and width % units == 0
        and width % (2 * CHUNK) == 0
        and devs % router[1] == 0
        and devs % NEAR == 0
    )


def body(mesh, *args):
    (
        hidden,
        query,
        keys,
        values,
        lengths,
        out_proj,
        gain,
        router,
        low_factor,
        gate_w,
        up_w,
        down_w,
        gate_low,
        up_low,
        experts,
    ) = args
    shapes = [x.shape for x in (hidden, query, keys, out_proj, router, gate_w)]
    if not fits(mesh, shapes):
        return plain_body(*args)
    devs, subs = mesh.shape["dev"], mesh.shape["sub"]
    rows, width = hidden.shape
    all_rows = devs * rows
    heads, hd = query.shape[1:]
    part = out_proj.shape[1] // subs
    units = gate_w.shape[1]
    rank = low_factor.shape[1]
    down_steps = width // (2 * CHUNK)
    total = 2 * (width // units) * (units // CHUNK) + 2 * down_steps
    slots = min(total, RING_BYTES // (units * CHUNK * 2))
    anywhere = pl.BlockSpec(memory_space=pl.ANY)
    vmem = pl.BlockSpec(memory_space=pltpu.VMEM)
    smem = pl.BlockSpec(memory_space=pltpu.SMEM)
    dma = pltpu.SemaphoreType.DMA
    scratch = [
        pltpu.VMEM((slots, units, CHUNK), BF16),
        pltpu.VMEM(hidden.shape, BF16),
        pltpu.VMEM(query.shape, BF16),
        pltpu.VMEM(keys.shape, BF16),
        pltpu.VMEM(values.shape, BF16),
        pltpu.VMEM(out_proj.shape, BF16),
        pltpu.VMEM(low_factor.shape, BF16),
        pltpu.VMEM(gate_low.shape, BF16),
        pltpu.VMEM(up_low.shape, BF16),
        pltpu.VMEM((heads, rows, hd), F32),
        pltpu.VMEM((devs, rows, heads * hd), BF16),
        pltpu.VMEM((devs, rows, part), BF16),
        pltpu.VMEM((devs, rows, 128), jnp.int32),
        pltpu.VMEM((all_rows, part), F32),
        pltpu.VMEM((all_rows, part), F32),
        pltpu.VMEM((devs * subs, all_rows, part), BF16),
        pltpu.VMEM((all_rows, width), F32),
        pltpu.VMEM((all_rows, width), BF16),
        pltpu.VMEM((all_rows, rank), F32),
        pltpu.VMEM((all_rows, rank), F32),
        pltpu.VMEM((all_rows, units), BF16),
        pltpu.VMEM((2, all_rows, CHUNK), F32),
        pltpu.VMEM((down_steps, all_rows, CHUNK), BF16),
        pltpu.VMEM((down_steps, all_rows, CHUNK), BF16),
        pltpu.VMEM((down_steps, devs, rows, CHUNK), BF16),
        pltpu.VMEM((down_steps, devs, rows, CHUNK), BF16),
        dma((slots,)),
        dma((8,)),
    ]
    scratch += [dma((devs,)) for _ in range(10)]
    scratch += [dma((2,)), dma((2,)), dma((down_steps,)), dma((down_steps,))]
    scratch += [dma((down_steps, devs)), dma((down_steps, devs))]
    scratch += [dma((down_steps,)), dma((down_steps,))]
    residual, mixture = pl.pallas_call(
        functools.partial(layer_kernel, devs, subs, slots),
        out_shape=(
            jax.ShapeDtypeStruct((rows, width), F32),
            jax.ShapeDtypeStruct((rows, width), F32),
        ),
        in_specs=[anywhere] * 4
        + [smem, anywhere, vmem, vmem]
        + [anywhere] * 6
        + [smem],
        out_specs=(vmem, vmem),
        scratch_shapes=scratch,
        compiler_params=pltpu.CompilerParams(
            collective_id=0, has_side_effects=True, vmem_limit_bytes=VMEM_BYTES
        ),
    )(
        hidden,
        query,
        keys,
        values,
        lengths,
        out_proj,
        gain.reshape(1, width),
        router.T,
        low_factor,
        gate_w,
        up_w,
        down_w,
        gate_low,
        up_low,
        experts.T,
    )
    return pl.pallas_call(
        add_kernel,
        out_shape=(
            jax.ShapeDtypeStruct((rows, width), BF16),
            jax.ShapeDtypeStruct((rows, width), F32),
        ),
        in_specs=[vmem, vmem],
        out_specs=(vmem, vmem),
    )(residual, mixture)


def solution(mesh):
    placed = (
        P(("groups", "dev"), None),
        P(("groups", "dev"), "sub", None),
        P(("groups", "dev"), "sub", None, None),
        P(("groups", "dev"), "sub", None, None),
        P(("groups", "dev")),
        P("sub", "dev"),
        P(),
        P(),
        P("sub", None),
        P(None, ("dev", "sub")),
        P(None, ("dev", "sub")),
        P(("dev", "sub"), None),
        P(None, ("dev", "sub")),
        P(None, ("dev", "sub")),
        P(("groups", "dev"), None),
    )
    return jax.shard_map(
        functools.partial(body, mesh),
        mesh=mesh,
        in_specs=placed,
        out_specs=(P(("groups", "dev"), None), P(("groups", "dev"), None)),
        check_vma=False,
    )
```
